256 devices in a mesh: blk: 32 (over y_lo, z, core), ffn: 8 (over y_hi, x).
Axes of the slice: x: 4, y: 4 (y_hi: 2, y_lo: 2; y = y_hi * 2 + y_lo), z: 8, core: 2. Of those that a mesh axis runs over, the one named last changes fastest.
Arguments:
- tokens: bfloat16 [8192, 4608], P('blk'), may hold values from -6 to 6
- ln_gain: float32 [4608], replicated, may hold values from 0.5 to 2
- ln_bias: float32 [4608], replicated, may hold values from -3 to 3
- fc1_tiles: bfloat16 [32, 8, 12, 128, 128], P('blk', 'ffn'), may hold values from -0.125 to 0.125
- fc1_index: int32 [32, 8, 12], P('blk', 'ffn'), may hold values from 0 to 647, as said below
- fc1_count: int32 [32, 8], P('blk', 'ffn'), may hold values from 7 to 12, as said below
- fc1_bias: float32 [18432], P('ffn'), may hold values from -3 to 3
- fc2_tiles: bfloat16 [32, 8, 12, 128, 128], P('blk', 'ffn'), may hold values from -0.09375 to 0.09375
- fc2_index: int32 [32, 8, 12], P('blk', 'ffn'), may hold values from 0 to 647, as said below
- fc2_count: int32 [32, 8], P('blk', 'ffn'), may hold values from 7 to 12, as said below
- fc2_bias: float32 [4608], P('ffn'), may hold values from -3 to 3
Outputs:
- result: bfloat16 [8192, 4608], P('blk', 'ffn')
The draws below stay inside these ranges and needn't reach their ends.
Inputs may be any that keep to these rules, and one draw needn't show every extreme that they name: `fc1_index`: within one index f of ffn, the positions of all live slots (s < the shard's count) are distinct. `fc2_index`: as for fc1_index. `fc1_count`: some shard of every index of ffn has all 12 slots live. `fc2_count`: as for fc1_count.
All inputs are finite; a program needn't handle non-finite values.
Results may differ from the reference program's by a relative error of at most 0.01.
Values may be sent and summed in bfloat16 or wider, within the bound.
A program may use at most 128 MiB of HBM per device.

```python
import math
import jax
import jax.numpy as jnp
from jax import lax

D = 4608
FF = 18432
TB = 128
TOKENS = 8192
RB = 36
FFS = 2304
CB = 18
MEAN_TILES = 10
SLOTS = 12
N_BLK = 32
N_FFN = 8


def tile_layout(key, salt):
    base = jax.random.fold_in(key, salt)
    key_counts, key_top, key_perm = jax.random.split(base, 3)
    lowest = MEAN_TILES * 3 // 4
    counts = jax.random.randint(key_counts, (N_BLK, N_FFN), lowest, SLOTS + 1)
    top_row = jax.random.randint(key_top, (N_FFN,), 0, N_BLK)
    low_row = (top_row + 1) % N_BLK
    shard_ids = jnp.arange(N_BLK)[:, None]
    counts = jnp.where(shard_ids == top_row[None, :], SLOTS, counts)
    counts = jnp.where(shard_ids == low_row[None, :], lowest, counts)
    starts = jnp.cumsum(counts, axis=0) - counts
    perm_keys = jax.random.split(key_perm, N_FFN)
    perms = jax.vmap(lambda one_key: jax.random.permutation(one_key, RB * CB))(perm_keys)
    rotate = RB * CB - 1 - perms[:, 0:1]
    perms = (perms + rotate) % (RB * CB)
    offsets = jnp.minimum(starts[:, :, None] + jnp.arange(SLOTS)[None, None, :], RB * CB - 1)
    groups = jnp.arange(N_FFN)[None, :, None]
    positions = perms[groups, offsets]
    return (positions.astype(jnp.int32), counts.astype(jnp.int32))


def draw_fc1_index(key, part):
    return tile_layout(key, 11)[0]


def draw_fc1_count(key, part):
    return tile_layout(key, 11)[1]


def draw_fc2_index(key, part):
    return tile_layout(key, 23)[0]


def draw_fc2_count(key, part):
    return tile_layout(key, 23)[1]


def level_of(key, dims, shards, low, largest):
    loudness = 1.0
    for dim, shards_of in shards:
        heights = jax.random.uniform(jax.random.fold_in(jax.random.fold_in(key, 6), dim), (shards_of,), jnp.float32, low / len(shards), largest / len(shards))
        loudness = loudness * jnp.repeat(jnp.exp(heights), dims[dim] // shards_of).reshape((-1,) + (1,) * (len(dims) - 1 - dim))
    return loudness


def scatter_about(stream_key, dims, scale, most, cuts=(), held_as=jnp.bfloat16):
    factor_of = level_of(stream_key, dims, cuts, -0.22, 0.18) if cuts else 1.0
    values = jax.random.normal(stream_key, dims, jnp.float32) * scale * factor_of
    return jnp.minimum(jnp.maximum(values, -most), most).astype(held_as)


def setup_inputs(seed: int = 0) -> dict:
    splits = jax.random.split(jax.random.key(seed), 12)
    tokens = scatter_about(splits[0], (TOKENS, D), 1.0, 6.0, ((0, 32),))
    ln_gain = jnp.clip(jnp.exp(jax.random.uniform(splits[1], (D,), jnp.float32, math.log(0.5), math.log(2.0))), 0.5, 2.0)
    ln_bias = scatter_about(splits[2], (D,), 0.5, 3.0, (), jnp.float32)
    fc1_tiles = scatter_about(splits[3], (N_BLK, N_FFN, SLOTS, TB, TB), (D // 2) ** -0.5, 0.125, ((0, 32), (1, 8)))
    fc1_index = draw_fc1_index(jax.random.fold_in(splits[11], 71), 0)
    fc1_count = draw_fc1_count(jax.random.fold_in(splits[11], 71), 0)
    fc1_bias = scatter_about(splits[6], (FF,), 0.5, 3.0, ((0, 8),), jnp.float32)
    fc2_tiles = scatter_about(splits[7], (N_BLK, N_FFN, SLOTS, TB, TB), (FF // 4) ** -0.5, 0.09375, ((0, 32), (1, 8)))
    fc2_index = draw_fc2_index(jax.random.fold_in(splits[11], 71), 0)
    fc2_count = draw_fc2_count(jax.random.fold_in(splits[11], 71), 0)
    fc2_bias = scatter_about(splits[10], (D,), 0.5, 3.0, ((0, 8),), jnp.float32)
    return {"tokens": tokens, "ln_gain": ln_gain, "ln_bias": ln_bias, "fc1_tiles": fc1_tiles, "fc1_index": fc1_index, "fc1_count": fc1_count, "fc1_bias": fc1_bias, "fc2_tiles": fc2_tiles, "fc2_index": fc2_index, "fc2_count": fc2_count, "fc2_bias": fc2_bias}


def dense_group(tile_data, slot_pos, live_count, group, rows, cols):
    flat = tile_data[:, group].reshape(N_BLK * SLOTS, TB, TB).astype(jnp.float32)
    alive = (jnp.arange(SLOTS)[None, :] < live_count[:, group][:, None]).reshape(-1)
    places = slot_pos[:, group].reshape(-1).astype(jnp.int32)
    grid = jnp.zeros((rows * cols, TB, TB), jnp.float32)
    grid = grid.at[places].add(jnp.where(alive[:, None, None], flat, jnp.float32(0.0)))
    grid = grid.reshape(rows, cols, TB, TB).transpose(0, 2, 1, 3).reshape(rows * TB, cols * TB)
    return grid.astype(jnp.bfloat16)

def reference(tokens, ln_gain, ln_bias, fc1_tiles, fc1_index, fc1_count, fc1_bias, fc2_tiles, fc2_index, fc2_count, fc2_bias):
    rows_f = tokens.astype(jnp.float32)
    center = lax.optimization_barrier(jnp.mean(rows_f, axis=1, keepdims=True))
    spread = lax.optimization_barrier(jnp.mean((rows_f - center) ** 2, axis=1, keepdims=True))
    normed = ((rows_f - center) / jnp.sqrt(spread + 1e-05) * ln_gain + ln_bias).astype(jnp.bfloat16)
    branch = jnp.zeros((TOKENS, D), jnp.float32)
    for group in range(N_FFN):
        first = dense_group(fc1_tiles, fc1_index, fc1_count, group, RB, CB)
        hidden = jnp.dot(normed, first, preferred_element_type=jnp.float32) + fc1_bias[group * FFS:(group + 1) * FFS]
        hidden = jnp.maximum(hidden, 0.0).astype(jnp.bfloat16)
        second = dense_group(fc2_tiles, fc2_index, fc2_count, group, CB, RB)
        partial_f = jnp.dot(hidden, second, preferred_element_type=jnp.float32).astype(jnp.bfloat16)
        branch = branch + partial_f.astype(jnp.float32)
    return (rows_f + branch + fc2_bias).astype(jnp.bfloat16)
```

```python
import jax
import jax.numpy as jnp
from jax import lax
from jax.experimental import pallas as pl
from jax.experimental.pallas import tpu as pltpu
from jax.sharding import PartitionSpec as P

MESH = pl.DeviceIdType.MESH
TB = 128
SLOTS = 12
NP, NQ = 7, 5
ROWS, D, FFS = 256, 4608, 2304
RB, CB = 36, 18
SW = 640
TOT = 32 * SLOTS
F32, BF16 = jnp.float32, jnp.bfloat16


def kernel(
    tok_h, gain, beta, b1, b2, t1, t2, meta, out,
    G1, G2, M, Tv, Ts, tok, normed, hidden, S, R, RY,
    ls, ss, zA, zQ, yQ, yP, dS, mS, mY, mD, mZ, rS, rX, rY,
):
    b = lax.axis_index("blk")
    f = lax.axis_index("ffn")
    j, z, c = b // 16, (b // 2) % 8, b % 2
    yh, x = f // 4, f % 4
    tin, G = (t1, t2), (G1, G2)
    zdev = tuple({"blk": j * 16 + ((z + dz) % 8) * 2 + c} for dz in (1, 7))
    ydev = {"blk": (1 - j) * 16 + z * 2 + c}
    ddev = {"blk": j * 16 + z * 2 + (1 - c)}
    xdev = tuple({"ffn": yh * 4 + (x + dx) % 4} for dx in (1, 3))
    hdev = {"ffn": (1 - yh) * 4 + x}

    bar = pltpu.get_barrier_semaphore()
    for dev in (*zdev, ydev, ddev, *xdev, hdev):
        pl.semaphore_signal(bar, inc=1, device_id=dev, device_id_type=MESH)
    tok_cp = pltpu.make_async_copy(tok_h, tok, ls.at[2])
    tok_cp.start()
    pl.semaphore_wait(bar, 7)

    def send(src, dst, s_sem, r_sem, dev):
        pltpu.make_async_remote_copy(
            src_ref=src, dst_ref=dst, send_sem=s_sem, recv_sem=r_sem,
            device_id=dev, device_id_type=MESH,
        ).start()

    def got(ref, s_sem, r_sem, dev):
        pltpu.make_async_remote_copy(
            src_ref=ref, dst_ref=ref, send_sem=s_sem, recv_sem=r_sem,
            device_id=dev, device_id_type=MESH,
        ).wait_recv()

    def base(cc, jj, zz):
        return (cc * 16 + jj * 8 + zz) * SLOTS

    own = base(c, j, z)

    def start(q):
        g, t = G[q], tin[q]
        pltpu.make_async_copy(t, g.at[pl.ds(own, SLOTS)], ls.at[q]).start()
        for d in (0, 1):
            send(t, g.at[pl.ds(own, SLOTS)], ss.at[q], zA.at[q, d, 0], zdev[d])
        send(t.at[pl.ds(NP, NQ)], g.at[pl.ds(own + NP, NQ)], ss.at[q], yQ.at[q], ydev)
        send(t.at[pl.ds(0, NP)], g.at[pl.ds(own, NP)], ss.at[q], yP.at[q, 0], ydev)
        send(t, g.at[pl.ds(own, SLOTS)], ss.at[q], dS.at[q], ddev)

    def origin(d, s):
        return (z + (8 - s if d == 0 else s)) % 8

    def fwd(q, lo, n, r_sem, dev):
        ref = G[q].at[pl.ds(lo, n)]
        send(ref, ref, ss.at[q], r_sem, dev)

    def arrived(q, lo, n, r_sem, dev):
        got(G[q].at[pl.ds(lo, n)], ss.at[q], r_sem, dev)

    def relay(q, s):
        if s == 1:
            lo = base(c, 1 - j, z) + NP
            arrived(q, lo, NQ, yQ.at[q], ydev)
            for d in (0, 1):
                fwd(q, lo, NQ, zQ.at[q, d, 0], zdev[d])
            fwd(q, lo, NQ, dS.at[q], ddev)
        for d in (0, 1):
            lo = base(c, j, origin(d, s))
            if s < 4:
                arrived(q, lo, SLOTS, zA.at[q, d, s - 1], zdev[1 - d])
                if s < 3:
                    fwd(q, lo, SLOTS, zA.at[q, d, s], zdev[d])
                elif d == 0:
                    fwd(q, lo, NP, zA.at[q, d, s], zdev[d])
                else:
                    fwd(q, lo + NP, NQ, zA.at[q, d, s], zdev[d])
                fwd(q, lo, NP, yP.at[q, 2 * s - 1 + d], ydev)
                fwd(q, lo, SLOTS, dS.at[q], ddev)
            elif d == 0:
                arrived(q, lo, NP, zA.at[q, d, 3], zdev[1 - d])
                fwd(q, lo, NP, yP.at[q, 7], ydev)
                fwd(q, lo, NP, dS.at[q], ddev)
            else:
                arrived(q, lo + NP, NQ, zA.at[q, d, 3], zdev[1 - d])
                fwd(q, lo + NP, NQ, dS.at[q], ddev)
        for d in (0, 1):
            lo = base(c, 1 - j, origin(d, s)) + NP
            if s < 4:
                arrived(q, lo, NQ, zQ.at[q, d, s - 1], zdev[1 - d])
                if s < 3:
                    fwd(q, lo, NQ, zQ.at[q, d, s], zdev[d])
                elif d == 0:
                    fwd(q, lo, 2, zQ.at[q, d, s], zdev[d])
                else:
                    fwd(q, lo + 2, NQ - 2, zQ.at[q, d, s], zdev[d])
                fwd(q, lo, NQ, dS.at[q], ddev)
            elif d == 0:
                arrived(q, lo, 2, zQ.at[q, d, 3], zdev[1 - d])
                fwd(q, lo, 2, dS.at[q], ddev)
            else:
                arrived(q, lo + 2, NQ - 2, zQ.at[q, d, 3], zdev[1 - d])
                fwd(q, lo + 2, NQ - 2, dS.at[q], ddev)
        late = {1: ((0, 0),), 2: ((0, 1), (1, 1)), 3: ((0, 2), (1, 2)), 4: ((0, 3), (1, 3), (0, 4))}[s]
        for d, back in late:
            lo = base(c, 1 - j, origin(d, back) if back else z)
            arrived(q, lo, NP, yP.at[q, 2 * back - 1 + d if back else 0], ydev)
            fwd(q, lo, NP, dS.at[q], ddev)

    def m_at(zz, n=4):
        return M.at[pl.ds(zz * 4, n)]

    mine = M.at[pl.ds(z * 4 + c * 2 + j, 1)]
    pltpu.make_async_copy(meta, mine, ls.at[3]).start()
    send(meta, mine, mS, mY, ydev)
    start(0)
    pltpu.make_async_copy(meta, mine, ls.at[3]).wait()
    got(M.at[pl.ds(z * 4 + c * 2 + (1 - j), 1)], mS, mY, ydev)
    pair = M.at[pl.ds(z * 4 + c * 2, 2)]
    send(pair, pair, mS, mD, ddev)
    got(M.at[pl.ds(z * 4 + (1 - c) * 2, 2)], mS, mD, ddev)
    for d in (0, 1):
        send(m_at(z), m_at(z), mS, mZ.at[d, 0], zdev[d])

    def meta_relay(s):
        for d in (0, 1):
            if d == 1 and s == 4:
                continue
            at = m_at(origin(d, s))
            got(at, mS, mZ.at[d, s - 1], zdev[1 - d])
            if s + d < 4:
                send(at, at, mS, mZ.at[d, s], zdev[d])

    tok_cp.wait()

    def norm_rows(i, carry):
        rows = pl.ds(pl.multiple_of(i * 16, 16), 16)
        t = tok[rows, :].astype(F32)
        mu = jnp.mean(t, axis=1, keepdims=True)
        t = t - mu
        var = jnp.mean(t * t, axis=1, keepdims=True)
        normed[rows, :] = (t / jnp.sqrt(var + 1e-05) * gain[...] + beta[...]).astype(BF16)
        return carry

    lax.fori_loop(0, ROWS // 16, norm_rows, 0)
    zero_tile = jnp.zeros((TB, TB), BF16)
    G1[TOT] = zero_tile
    G2[TOT] = zero_tile

    relay(0, 1)
    meta_relay(1)
    relay(0, 2)
    meta_relay(2)
    relay(0, 3)
    start(1)
    meta_relay(3)
    meta_relay(4)

    m_id = lax.broadcasted_iota(jnp.int32, (32, TB), 0)
    first = ((m_id // 2 % 2) * 16 + (m_id % 2) * 8 + m_id // 4) * SLOTS
    lane = lax.broadcasted_iota(jnp.int32, (32, TB), 1)
    for q, (nr, nc) in enumerate(((RB, CB), (CB, RB))):
        seen = M[:, q, :]

        def row(r, carry):
            want = jnp.where(lane < nc, r * nc + lane, -2)
            best = jnp.full((32, TB), -1, jnp.int32)
            for s in range(SLOTS):
                best = jnp.where(seen[:, s : s + 1] == want, first + s, best)
            best = jnp.max(best, axis=0, keepdims=True)
            Tv[q, pl.ds(r, 1), :] = jnp.where(best < 0, TOT, best)
            return carry

        lax.fori_loop(0, nr, row, 0)
    tab_cp = pltpu.make_async_copy(Tv, Ts, ls.at[4])
    tab_cp.start()
    relay(0, 4)
    pltpu.make_async_copy(t1, G1.at[pl.ds(own, SLOTS)], ls.at[0]).wait()
    arrived(0, base(1 - c, 0, 0), TOT // 2, dS.at[0], ddev)
    tab_cp.wait()

    def block(g, q, r, col, wide):
        cols = []
        for w in range(wide):
            cols.append(jnp.concatenate([g[Ts[q, r, col + w]], g[Ts[q, r + 1, col + w]]], axis=0))
        return cols[0] if wide == 1 else jnp.concatenate(cols, axis=1)

    def product(src, g, q, chunks, col, wide):
        acc = None
        for k in range(chunks):
            part = jnp.dot(
                src[:, k * 256 : (k + 1) * 256], block(g, q, 2 * k, col, wide),
                preferred_element_type=F32,
            )
            acc = part if acc is None else acc + part
        return acc

    def fc1(p, carry):
        acc = product(normed, G1, 0, RB // 2, 2 * p, 2)
        cols = pl.ds(pl.multiple_of(p * 256, 256), 256)
        hidden[:, cols] = jnp.maximum(acc + b1[:, cols], 0.0).astype(BF16)
        return carry

    lax.fori_loop(0, 4, fc1, 0)
    relay(1, 1)
    lax.fori_loop(4, 9, fc1, 0)
    relay(1, 2)
    relay(1, 3)
    relay(1, 4)
    pltpu.make_async_copy(t2, G2.at[pl.ds(own, SLOTS)], ls.at[1]).wait()
    arrived(1, base(1 - c, 0, 0), TOT // 2, dS.at[1], ddev)

    def fc2(i, carry):
        d, step = i % 2, i // 2
        share = d * 4 + (x + 1 + step + (1 - d) * (2 - 2 * step)) % 4
        col = share // 2 * 9 + share % 2 * 4
        for w, wide in ((0, 2), (2, 2), (4, 1)):
            acc = product(hidden, G2, 1, CB // 2, col + w, wide)
            S[i, :, w * TB : (w + wide) * TB] = acc.astype(BF16)
        return carry

    H = ROWS // 2

    def ring(step):
        for h in (0, 1):
            for d in (0, 1):
                at = S.at[2 * step + d, pl.ds(h * H, H)]
                if step:
                    old = R.at[d, step - 1, pl.ds(h * H, H)]
                    got(old, rS, rX.at[d, step - 1, h], xdev[1 - d])
                    at[...] = (at[...].astype(F32) + old[...].astype(F32)).astype(BF16)
                send(at, R.at[d, step, pl.ds(h * H, H)], rS, rX.at[d, step, h], xdev[d])

    lax.fori_loop(0, 2, fc2, 0)
    ring(0)
    lax.fori_loop(2, 6, fc2, 0)
    ring(1)
    lax.fori_loop(6, 8, fc2, 0)
    ring(2)
    o = 1 - yh
    for h in (0, 1):
        rows = pl.ds(h * H, H)
        at, old = S.at[6 + o, rows], R.at[o, 2, rows]
        got(old, rS, rX.at[o, 2, h], xdev[0])
        at[...] = (at[...].astype(F32) + old[...].astype(F32)).astype(BF16)
        send(at, RY.at[rows], rS, rY.at[h], hdev)
    lo = pl.multiple_of((f // 2 * 9 + f % 2 * 4) * TB, TB)
    for h in (0, 1):
        rows = pl.ds(h * H, H)
        got(R.at[yh, 2, rows], rS, rX.at[yh, 2, h], xdev[0])
        got(RY.at[rows], rS, rY.at[h], hdev)
        sum_ = S[6 + yh, rows].astype(F32) + R[yh, 2, rows].astype(F32) + RY[rows].astype(F32)
        sum_ = sum_ + tok[rows, pl.ds(lo, SW)].astype(F32)

        @pl.when(f % 2 == 0)
        def _():
            out[rows, :] = (sum_[:, :576] + b2[...]).astype(BF16)

        @pl.when(f % 2 == 1)
        def _():
            out[rows, :] = (sum_[:, SW - 576 :] + b2[...]).astype(BF16)

    for q in (0, 1):
        all_sent = G[q].at[pl.ds(0, 372)]
        pltpu.make_async_remote_copy(
            src_ref=all_sent, dst_ref=all_sent, send_sem=ss.at[q], recv_sem=ss.at[q],
            device_id=ddev, device_id_type=MESH,
        ).wait_send()
    sent = S.at[pl.ds(0, 7)]
    pltpu.make_async_remote_copy(
        src_ref=sent, dst_ref=sent, send_sem=rS, recv_sem=rS, device_id=ddev, device_id_type=MESH,
    ).wait_send()
    for ref in (M.at[pl.ds(0, 31)],):
        pltpu.make_async_remote_copy(
            src_ref=ref, dst_ref=ref, send_sem=mS, recv_sem=mS, device_id=ddev, device_id_type=MESH,
        ).wait_send()


def on_device(tokens, gain, beta, t1, i1, n1, b1, t2, i2, n2, b2):
    def listed(index, count):
        live = jnp.arange(SLOTS, dtype=jnp.int32) < count.reshape(1)
        return jnp.pad(jnp.where(live, index.reshape(SLOTS), -1), (0, TB - SLOTS), constant_values=-1)

    meta = jnp.pad(jnp.stack([listed(i1, n1), listed(i2, n2)]), ((0, 6), (0, 0)))[None]
    vm = pl.BlockSpec(memory_space=pltpu.VMEM)
    hb = pl.BlockSpec(memory_space=pl.ANY)
    dma, V = pltpu.SemaphoreType.DMA, pltpu.VMEM
    return pl.pallas_call(
        kernel,
        out_shape=jax.ShapeDtypeStruct((ROWS, 576), BF16),
        in_specs=[hb, vm, vm, vm, vm, hb, hb, hb],
        out_specs=vm,
        scratch_shapes=[
            V((TOT + 1, TB, TB), BF16),
            V((TOT + 1, TB, TB), BF16),
            V((32, 8, TB), jnp.int32),
            V((2, 40, TB), jnp.int32),
            pltpu.SMEM((2, 40, TB), jnp.int32),
            V((ROWS, D), BF16),
            V((ROWS, D), BF16),
            V((ROWS, FFS), BF16),
            V((8, ROWS, SW), BF16),
            V((2, 3, ROWS, SW), BF16),
            V((ROWS, SW), BF16),
            dma((5,)),
            dma((2,)),
            dma((2, 2, 4)),
            dma((2, 2, 4)),
            dma((2,)),
            dma((2, 8)),
            dma((2,)),
            dma,
            dma,
            dma,
            dma((2, 4)),
            dma,
            dma((2, 3, 2)),
            dma((2,)),
        ],
        compiler_params=pltpu.CompilerParams(
            collective_id=0, has_side_effects=True, vmem_limit_bytes=60 * 1024 * 1024
        ),
    )(
        tokens, gain.reshape(1, D), beta.reshape(1, D), b1.reshape(1, FFS), b2.reshape(1, 576),
        t1.reshape(SLOTS, TB, TB), t2.reshape(SLOTS, TB, TB), meta,
    )


def solution(mesh):
    tile, pair = P("blk", "ffn", None, None, None), P("blk", "ffn")
    placed = (
        P("blk", None), P(), P(), tile, P("blk", "ffn", None), pair, P("ffn"),
        tile, P("blk", "ffn", None), pair, P("ffn"),
    )
    return jax.shard_map(
        on_device, mesh=mesh, in_specs=placed, out_specs=P("blk", "ffn"), check_vma=False
    )
```

```python
import jax
import jax.numpy as jnp
from jax import lax
from jax.experimental import pallas as pl
from jax.experimental.pallas import tpu as pltpu
from jax.sharding import PartitionSpec as P

MESH = pl.DeviceIdType.MESH
TB = 128
SLOTS = 12
NP, NQ = 7, 5
FAR = (2, 3)
ROWS, D, FFS = 256, 4608, 2304
RB, CB = 36, 18
SW = 640
SR = 1152
TOT = 32 * SLOTS
F32, BF16 = jnp.float32, jnp.bfloat16


def kernel(
    tok_h, gain, beta, b1, b2, t1, t2, i1, n1, i2, n2, out,
    G1, G2, M, Tv, Ts, tok, normed, hidden, S, R, RY, W,
    ls, ss, zA, zQ, yQ, yP, dS, mS, mY, mD, mZ, rS, rX, rY,
):
    b = lax.axis_index("blk")
    f = lax.axis_index("ffn")
    j, z, c = b // 16, (b // 2) % 8, b % 2
    yh, x = f // 4, f % 4
    tin, G = (t1, t2), (G1, G2)
    zdev = tuple({"blk": j * 16 + ((z + dz) % 8) * 2 + c} for dz in (1, 7))
    ydev = {"blk": (1 - j) * 16 + z * 2 + c}
    ddev = {"blk": j * 16 + z * 2 + (1 - c)}
    xdev = tuple({"ffn": yh * 4 + (x + dx) % 4} for dx in (1, 3))
    hdev = {"ffn": (1 - yh) * 4 + x}

    bar = pltpu.get_barrier_semaphore()
    for dev in (*zdev, ydev, ddev, *xdev, hdev):
        pl.semaphore_signal(bar, inc=1, device_id=dev, device_id_type=MESH)
    tok_cp = pltpu.make_async_copy(tok_h, tok, ls.at[2])
    tok_cp.start()
    sub = lax.broadcasted_iota(jnp.int32, (8, TB), 0)
    lane8 = lax.broadcasted_iota(jnp.int32, (8, TB), 1)
    seen = jnp.full((8, TB), -1, jnp.int32)
    for q, (idx, num) in enumerate(((i1, n1), (i2, n2))):
        for s in range(SLOTS):
            here = (sub == q) & (lane8 == s) & (s < num[0, 0])
            seen = jnp.where(here, idx[0, 0, s], seen)
    M[z * 4 + c * 2 + j] = seen
    pl.semaphore_wait(bar, 7)

    def send(src, dst, s_sem, r_sem, dev):
        pltpu.make_async_remote_copy(
            src_ref=src, dst_ref=dst, send_sem=s_sem, recv_sem=r_sem,
            device_id=dev, device_id_type=MESH,
        ).start()

    def got(ref, s_sem, r_sem, dev):
        pltpu.make_async_remote_copy(
            src_ref=ref, dst_ref=ref, send_sem=s_sem, recv_sem=r_sem,
            device_id=dev, device_id_type=MESH,
        ).wait_recv()

    def base(cc, jj, zz):
        return (cc * 16 + jj * 8 + zz) * SLOTS

    own = base(c, j, z)

    def start_y(q):
        g, t = G[q], tin[q]
        send(t.at[pl.ds(NP, NQ)], g.at[pl.ds(own + NP, NQ)], ss.at[q], yQ.at[q], ydev)
        send(t.at[pl.ds(0, NP)], g.at[pl.ds(own, NP)], ss.at[q], yP.at[q, 0], ydev)

    def start_z(q):
        g, t = G[q], tin[q]
        for k, (lo, n) in enumerate(((0, NP), (NP, NQ))):
            for d in (0, 1):
                send(t.at[pl.ds(lo, n)], g.at[pl.ds(own + lo, n)], ss.at[q], zA.at[q, d, 0, k], zdev[d])
        send(t, g.at[pl.ds(own, SLOTS)], ss.at[q], dS.at[q], ddev)
        pltpu.make_async_copy(t, g.at[pl.ds(own, SLOTS)], ls.at[q]).start()

    def origin(d, s):
        return (z + (8 - s if d == 0 else s)) % 8

    def fwd(q, lo, n, r_sem, dev):
        ref = G[q].at[pl.ds(lo, n)]
        send(ref, ref, ss.at[q], r_sem, dev)

    def arrived(q, lo, n, r_sem, dev):
        got(G[q].at[pl.ds(lo, n)], ss.at[q], r_sem, dev)

    def a_part(q, d, s, k):
        lo, n = base(c, j, origin(d, s)) + (NP if k else 0), (NQ if k else NP)
        arrived(q, lo, n, zA.at[q, d, s - 1, k], zdev[1 - d])
        if s < 3 or (s == 3 and d == k):
            fwd(q, lo, n, zA.at[q, d, s, k], zdev[d])
        if not k:
            fwd(q, lo, n, yP.at[q, 2 * s - 1 + d], ydev)
        fwd(q, lo, n, dS.at[q], ddev)

    def a_step(q, s):
        for k in (0, 1):
            for d in (0, 1):
                if s < 4 or d == k:
                    a_part(q, d, s, k)

    def q_at(d, s, half):
        lo = base(c, 1 - j, origin(d, s)) + NP
        if half is None:
            return lo, NQ
        return (lo, FAR[0]) if d != half else (lo + FAR[0], FAR[1])

    def q_own(q):
        lo = base(c, 1 - j, z) + NP
        for d in (0, 1):
            fwd(q, lo, NQ, zQ.at[q, d, 0, 0], zdev[d])

    def q_step(q, s):
        for half in (1, 0) if s == 3 else (1,) if s == 4 else (None,):
            for d in (0, 1):
                lo, n = q_at(d, s, half)
                arrived(q, lo, n, zQ.at[q, d, s - 1, 1 if half == 0 else 0], zdev[1 - d])
                if s == 1:
                    fwd(q, lo, n, zQ.at[q, d, 1, 0], zdev[d])
                if s == 2:
                    for h in (1, 0):
                        lo2, n2 = q_at(d, s, h)
                        fwd(q, lo2, n2, zQ.at[q, d, 2, 1 - h], zdev[d])
                if s == 3 and half == 1:
                    fwd(q, lo, n, zQ.at[q, d, 3, 0], zdev[d])
                fwd(q, lo, n, dS.at[q], ddev)

    def y_q(q):
        lo = base(c, 1 - j, z) + NP
        arrived(q, lo, NQ, yQ.at[q], ydev)
        fwd(q, lo, NQ, dS.at[q], ddev)

    def y_p(q, d, back):
        lo = base(c, 1 - j, origin(d, back) if back else z)
        arrived(q, lo, NP, yP.at[q, 2 * back - 1 + d if back else 0], ydev)
        fwd(q, lo, NP, dS.at[q], ddev)

    def m_at(zz, n=4):
        return M.at[pl.ds(zz * 4, n)]

    at = pl.ds(z * 4 + c * 2 + j, 1)
    send(M.at[at], M.at[at], mS, mY, ydev)
    start_y(0)
    start_z(0)
    got(M.at[pl.ds(z * 4 + c * 2 + (1 - j), 1)], mS, mY, ydev)
    both = M.at[pl.ds(z * 4 + c * 2, 2)]
    send(both, both, mS, mD, ddev)
    got(M.at[pl.ds(z * 4 + (1 - c) * 2, 2)], mS, mD, ddev)
    for d in (0, 1):
        send(m_at(z), m_at(z), mS, mZ.at[d, 0], zdev[d])

    def meta_relay(s):
        for d in (0, 1):
            if d == 1 and s == 4:
                continue
            at = m_at(origin(d, s))
            got(at, mS, mZ.at[d, s - 1], zdev[1 - d])
            if s + d < 4:
                send(at, at, mS, mZ.at[d, s], zdev[d])

    tok_cp.wait()

    def norm_rows(i, carry):
        rows = pl.ds(pl.multiple_of(i * 16, 16), 16)
        t = tok[rows, :].astype(F32)
        t = t - jnp.mean(t, axis=1, keepdims=True)
        var = jnp.mean(t * t, axis=1, keepdims=True)
        t = t * (1.0 / jnp.sqrt(var + 1e-05))
        normed[rows, :] = (t * gain[...][None] + beta[...][None]).astype(BF16)
        return carry

    lax.fori_loop(0, ROWS // 16, norm_rows, 0)
    zero_tile = jnp.zeros((TB, TB), BF16)
    G1[TOT] = zero_tile
    G2[TOT] = zero_tile

    y_q(0)
    a_step(0, 1)
    q_own(0)
    meta_relay(1)
    y_p(0, 0, 0)
    a_step(0, 2)
    meta_relay(2)
    q_step(0, 1)
    y_p(0, 0, 1)
    y_p(0, 1, 1)
    a_step(0, 3)
    start_y(1)
    meta_relay(3)
    q_step(0, 2)
    y_p(0, 0, 2)
    y_p(0, 1, 2)
    a_step(0, 4)
    start_z(1)
    meta_relay(4)

    m_id = lax.broadcasted_iota(jnp.int32, (32, TB), 0)
    first = ((m_id // 2 % 2) * 16 + (m_id % 2) * 8 + m_id // 4) * SLOTS
    lane = lax.broadcasted_iota(jnp.int32, (32, TB), 1)
    for q, (nr, nc) in enumerate(((RB, CB), (CB, RB))):
        listed = M[:, q, :]
        for s in range(SLOTS):
            W[s] = jnp.broadcast_to(listed[:, s : s + 1], (32, TB))

        def row(r, carry):
            want = jnp.where(lane < nc, r * nc + lane, -2)
            best = jnp.full((32, TB), -1, jnp.int32)
            for s in range(SLOTS):
                best = jnp.where(W[s] == want, first + s, best)
            best = jnp.max(best, axis=0, keepdims=True)
            Tv[q, pl.ds(r, 1), :] = jnp.where(best < 0, TOT, best)
            return carry

        lax.fori_loop(0, nr, row, 0)
    tab_cp = pltpu.make_async_copy(Tv, Ts, ls.at[4])
    tab_cp.start()
    q_step(0, 3)
    y_p(0, 0, 3)
    y_p(0, 1, 3)
    q_step(0, 4)
    y_p(0, 0, 4)
    y_q(1)
    pltpu.make_async_copy(t1, G1.at[pl.ds(own, SLOTS)], ls.at[0]).wait()
    arrived(0, base(1 - c, 0, 0), TOT // 2, dS.at[0], ddev)
    tab_cp.wait()

    def block(g, q, r, col, wide):
        cols = []
        for w in range(wide):
            cols.append(jnp.concatenate([g[Ts[q, r, col + w]], g[Ts[q, r + 1, col + w]]], axis=0))
        return cols[0] if wide == 1 else jnp.concatenate(cols, axis=1)

    def product(src, g, q, chunks, col, wide):
        acc = None
        for k in range(chunks):
            part = jnp.dot(
                src[:, k * 256 : (k + 1) * 256], block(g, q, 2 * k, col, wide),
                preferred_element_type=F32,
            )
            acc = part if acc is None else acc + part
        return acc

    def fc1(p, carry):
        acc = product(normed, G1, 0, RB // 2, 2 * p, 2)
        cols = pl.ds(pl.multiple_of(p * 256, 256), 256)
        hidden[:, cols] = jnp.maximum(acc + b1[cols][None], 0.0).astype(BF16)
        return carry

    a_step(1, 1)
    q_own(1)
    y_p(1, 0, 0)
    lax.fori_loop(0, 3, fc1, 0)
    a_step(1, 2)
    lax.fori_loop(3, 5, fc1, 0)
    q_step(1, 1)
    y_p(1, 0, 1)
    y_p(1, 1, 1)
    lax.fori_loop(5, 7, fc1, 0)
    a_step(1, 3)
    lax.fori_loop(7, 9, fc1, 0)
    q_step(1, 2)
    y_p(1, 0, 2)
    y_p(1, 1, 2)
    a_step(1, 4)
    q_step(1, 3)
    y_p(1, 0, 3)
    y_p(1, 1, 3)
    q_step(1, 4)
    y_p(1, 0, 4)
    pltpu.make_async_copy(t2, G2.at[pl.ds(own, SLOTS)], ls.at[1]).wait()
    arrived(1, base(1 - c, 0, 0), TOT // 2, dS.at[1], ddev)

    def fc2(i, carry):
        d, step = i % 2, i // 2
        share = d * 4 + (x + 1 + step + (1 - d) * (2 - 2 * step)) % 4
        pair, odd = share // 2 * 9, share % 2
        for w in (0, 2):
            acc = product(hidden, G2, 1, CB // 2, pair + odd * 5 + w, 2).astype(BF16)
            S[i, w * ROWS : (w + 1) * ROWS] = acc[:, :TB]
            S[i, (w + 1) * ROWS : (w + 2) * ROWS] = acc[:, TB:]
        acc = product(hidden, G2, 1, CB // 2, pair + 4, 1)
        top, low = acc[: ROWS // 2], acc[ROWS // 2 :]
        left = lax.broadcasted_iota(jnp.int32, (ROWS // 2, TB), 1) < TB // 2
        turned = pltpu.roll(jnp.where(odd == 1, top, low), TB // 2, 1)
        half = jnp.where(left == (odd == 1), turned, jnp.where(odd == 1, low, top))
        S[i, 4 * ROWS :] = half.astype(BF16)
        return carry

    H = SR // 2

    def ring(step):
        for h in (0, 1):
            for d in (0, 1):
                at = S.at[2 * step + d, pl.ds(h * H, H)]
                if step:
                    old = R.at[d, step - 1, pl.ds(h * H, H)]
                    got(old, rS, rX.at[d, step - 1, h], xdev[1 - d])
                    at[...] = (at[...].astype(F32) + old[...].astype(F32)).astype(BF16)
                send(at, R.at[d, step, pl.ds(h * H, H)], rS, rX.at[d, step, h], xdev[d])

    lax.fori_loop(0, 2, fc2, 0)
    ring(0)
    lax.fori_loop(2, 6, fc2, 0)
    ring(1)
    lax.fori_loop(6, 8, fc2, 0)
    ring(2)
    o = 1 - yh
    for h in (0, 1):
        rows = pl.ds(h * H, H)
        at, old = S.at[6 + o, rows], R.at[o, 2, rows]
        got(old, rS, rX.at[o, 2, h], xdev[0])
        at[...] = (at[...].astype(F32) + old[...].astype(F32)).astype(BF16)
        send(at, RY.at[rows], rS, rY.at[h], hdev)
    lo = pl.multiple_of((f // 2 * 9 + f % 2 * 4) * TB, TB)
    for h in (0, 1):
        rows = pl.ds(h * H, H)
        got(R.at[yh, 2, rows], rS, rX.at[yh, 2, h], xdev[0])
        got(RY.at[rows], rS, rY.at[h], hdev)
    total = S[6 + yh].astype(F32) + R[yh, 2].astype(F32) + RY[...].astype(F32)
    main = [total[w * ROWS : (w + 1) * ROWS] for w in range(4)]
    half = total[4 * ROWS :]
    turned = pltpu.roll(half, TB // 2, 1)

    @pl.when(f % 2 == 0)
    def _():
        full = jnp.concatenate(main + [jnp.concatenate([half, turned], axis=0)], axis=1)
        full = full + tok[:, pl.ds(lo, SW)].astype(F32)
        out[...] = (full[:, :576] + b2[...][None]).astype(BF16)

    @pl.when(f % 2 == 1)
    def _():
        full = jnp.concatenate([jnp.concatenate([turned, half], axis=0)] + main, axis=1)
        full = full + tok[:, pl.ds(lo, SW)].astype(F32)
        out[...] = (full[:, SW - 576 :] + b2[...][None]).astype(BF16)

    for q in (0, 1):
        all_sent = G[q].at[pl.ds(0, 372)]
        pltpu.make_async_remote_copy(
            src_ref=all_sent, dst_ref=all_sent, send_sem=ss.at[q], recv_sem=ss.at[q],
            device_id=ddev, device_id_type=MESH,
        ).wait_send()
    sent = S.at[pl.ds(0, 7)]
    pltpu.make_async_remote_copy(
        src_ref=sent, dst_ref=sent, send_sem=rS, recv_sem=rS, device_id=ddev, device_id_type=MESH,
    ).wait_send()
    ref = M.at[pl.ds(0, 31)]
    pltpu.make_async_remote_copy(
        src_ref=ref, dst_ref=ref, send_sem=mS, recv_sem=mS, device_id=ddev, device_id_type=MESH,
    ).wait_send()


def on_device(tokens, gain, beta, t1, i1, n1, b1, t2, i2, n2, b2):
    vm = pl.BlockSpec(memory_space=pltpu.VMEM)
    hb = pl.BlockSpec(memory_space=pl.ANY)
    sm = pl.BlockSpec(memory_space=pltpu.SMEM)
    dma, V = pltpu.SemaphoreType.DMA, pltpu.VMEM
    return pl.pallas_call(
        kernel,
        out_shape=jax.ShapeDtypeStruct((ROWS, 576), BF16),
        in_specs=[hb, vm, vm, vm, vm, hb, hb, sm, sm, sm, sm],
        out_specs=vm,
        scratch_shapes=[
            V((TOT + 1, TB, TB), BF16),
            V((TOT + 1, TB, TB), BF16),
            V((32, 8, TB), jnp.int32),
            V((2, 40, TB), jnp.int32),
            pltpu.SMEM((2, 40, TB), jnp.int32),
            V((ROWS, D), BF16),
            V((ROWS, D), BF16),
            V((ROWS, FFS), BF16),
            V((8, SR, TB), BF16),
            V((2, 3, SR, TB), BF16),
            V((SR, TB), BF16),
            V((SLOTS, 32, TB), jnp.int32),
            dma((5,)),
            dma((2,)),
            dma((2, 2, 4, 2)),
            dma((2, 2, 4, 2)),
            dma((2,)),
            dma((2, 8)),
            dma((2,)),
            dma,
            dma,
            dma,
            dma((2, 4)),
            dma,
            dma((2, 3, 2)),
            dma((2,)),
        ],
        compiler_params=pltpu.CompilerParams(
            collective_id=0, has_side_effects=True, vmem_limit_bytes=60 * 1024 * 1024
        ),
    )(
        tokens, gain, beta, b1, b2, t1.reshape(SLOTS, TB, TB), t2.reshape(SLOTS, TB, TB), i1, n1, i2, n2,
    )


def solution(mesh):
    tile, pair = P("blk", "ffn", None, None, None), P("blk", "ffn")
    placed = (
        P("blk", None), P(), P(), tile, P("blk", "ffn", None), pair, P("ffn"),
        tile, P("blk", "ffn", None), pair, P("ffn"),
    )
    return jax.shard_map(
        on_device, mesh=mesh, in_specs=placed, out_specs=P("blk", "ffn"), check_vma=False
    )
```

```python
import functools

import jax
import jax.numpy as jnp
from jax import lax
from jax.experimental import pallas as pl
from jax.experimental.pallas import tpu as pltpu
from jax.sharding import PartitionSpec as P

MESH = pl.DeviceIdType.MESH
TB = 128
SLOTS = 12
NP, NQ = 7, 5
FAR = (2, 3)
ROWS, D, FFS = 256, 4608, 2304
RB, CB = 36, 18
SW = 640
SR = 1152
SB = 512
TOT = 32 * SLOTS
F32, BF16 = jnp.float32, jnp.bfloat16


def kernel(
    tok_h, gain, beta, b1, b2, t1, t2, i1, c1, i2, c2, out,
    G1, G2, M, Tv, Ts, tok, normed, hidden, S, R, RY, YB, Q, W, n1, n2,
    ls, ss, zA, zQ, yQ, yP, dS, mS, mY, mD, mZ, rS, rX, rY, rB, rQ,
):
    b = lax.axis_index("blk")
    f = lax.axis_index("ffn")
    j, z, c = b // 16, (b // 2) % 8, b % 2
    yh, x = f // 4, f % 4
    tin, G = (t1, t2), (G1, G2)
    zdev = tuple({"blk": j * 16 + ((z + dz) % 8) * 2 + c} for dz in (1, 7))
    ydev = {"blk": (1 - j) * 16 + z * 2 + c}
    ddev = {"blk": j * 16 + z * 2 + (1 - c)}
    xdev = tuple({"ffn": yh * 4 + (x + dx) % 4} for dx in (1, 3))
    hdev = {"ffn": (1 - yh) * 4 + x}

    bar = pltpu.get_barrier_semaphore()
    for dev in (*zdev, ydev, ddev, *xdev, hdev):
        pl.semaphore_signal(bar, inc=1, device_id=dev, device_id_type=MESH)
    tok_cp = pltpu.make_async_copy(tok_h, tok, ls.at[2])
    tok_cp.start()
    counts = [pltpu.make_async_copy(h, num, ls.at[5 + k]) for k, (h, num) in enumerate(((c1, n1), (c2, n2)))]
    for cp in counts:
        cp.start()
    sub = lax.broadcasted_iota(jnp.int32, (8, TB), 0)
    lane8 = lax.broadcasted_iota(jnp.int32, (8, TB), 1)
    seen = jnp.full((8, TB), -1, jnp.int32)
    for cp in counts:
        cp.wait()
    for q, (idx, num) in enumerate(((i1, n1), (i2, n2))):
        for s in range(SLOTS):
            here = (sub == q) & (lane8 == s) & (s < num[0, 0])
            seen = jnp.where(here, idx[0, 0, s], seen)
    M[z * 4 + c * 2 + j] = seen
    pl.semaphore_wait(bar, 7)

    def send(src, dst, s_sem, r_sem, dev):
        pltpu.make_async_remote_copy(
            src_ref=src, dst_ref=dst, send_sem=s_sem, recv_sem=r_sem,
            device_id=dev, device_id_type=MESH,
        ).start()

    def got(ref, s_sem, r_sem, dev):
        pltpu.make_async_remote_copy(
            src_ref=ref, dst_ref=ref, send_sem=s_sem, recv_sem=r_sem,
            device_id=dev, device_id_type=MESH,
        ).wait_recv()

    def base(cc, jj, zz):
        return (cc * 16 + jj * 8 + zz) * SLOTS

    own = base(c, j, z)

    def start_y(q):
        g, t = G[q], tin[q]
        send(t.at[pl.ds(NP, NQ)], g.at[pl.ds(own + NP, NQ)], ss.at[q], yQ.at[q], ydev)
        send(t.at[pl.ds(0, NP)], g.at[pl.ds(own, NP)], ss.at[q], yP.at[q, 0], ydev)

    def start_z(q):
        g, t = G[q], tin[q]
        for k, (lo, n) in enumerate(((0, NP), (NP, NQ))):
            for d in (0, 1):
                send(t.at[pl.ds(lo, n)], g.at[pl.ds(own + lo, n)], ss.at[q], zA.at[q, d, 0, k], zdev[d])
        send(t, g.at[pl.ds(own, SLOTS)], ss.at[q], dS.at[q], ddev)
        pltpu.make_async_copy(t, g.at[pl.ds(own, SLOTS)], ls.at[q]).start()

    def origin(d, s):
        return (z + (8 - s if d == 0 else s)) % 8

    def fwd(q, lo, n, r_sem, dev):
        ref = G[q].at[pl.ds(lo, n)]
        send(ref, ref, ss.at[q], r_sem, dev)

    def arrived(q, lo, n, r_sem, dev):
        got(G[q].at[pl.ds(lo, n)], ss.at[q], r_sem, dev)

    def a_part(q, d, s, k):
        lo, n = base(c, j, origin(d, s)) + (NP if k else 0), (NQ if k else NP)
        far = ((lo, 4, 0), (lo + 4, n - 4, 1)) if d == k == 0 else ((lo, n, k),)
        if s == 4:
            for at, m, u in far:
                arrived(q, at, m, zA.at[q, d, 3, u], zdev[1 - d])
                if not k:
                    fwd(q, at, m, yP.at[q, 7 + u], ydev)
                fwd(q, at, m, dS.at[q], ddev)
            return
        arrived(q, lo, n, zA.at[q, d, s - 1, k], zdev[1 - d])
        if s < 3:
            fwd(q, lo, n, zA.at[q, d, s, k], zdev[d])
        elif d == k:
            for at, m, u in far:
                fwd(q, at, m, zA.at[q, d, 3, u], zdev[d])
        if not k:
            fwd(q, lo, n, yP.at[q, 2 * s - 1 + d], ydev)
        fwd(q, lo, n, dS.at[q], ddev)

    def a_step(q, s):
        for k in (0, 1):
            for d in (0, 1):
                if s < 4 or d == k:
                    a_part(q, d, s, k)

    def q_at(d, s, half):
        lo = base(c, 1 - j, origin(d, s)) + NP
        if half is None:
            return lo, NQ
        return (lo, FAR[0]) if d != half else (lo + FAR[0], FAR[1])

    def q_own(q):
        lo = base(c, 1 - j, z) + NP
        for d in (0, 1):
            fwd(q, lo, NQ, zQ.at[q, d, 0, 0], zdev[d])

    def q_step(q, s):
        for half in (1, 0) if s == 3 else (1,) if s == 4 else (None,):
            for d in (0, 1):
                lo, n = q_at(d, s, half)
                arrived(q, lo, n, zQ.at[q, d, s - 1, 1 if half == 0 else 0], zdev[1 - d])
                if s == 1:
                    fwd(q, lo, n, zQ.at[q, d, 1, 0], zdev[d])
                if s == 2:
                    for h in (1, 0):
                        lo2, n2 = q_at(d, s, h)
                        fwd(q, lo2, n2, zQ.at[q, d, 2, 1 - h], zdev[d])
                if s == 3 and half == 1:
                    fwd(q, lo, n, zQ.at[q, d, 3, 0], zdev[d])
                fwd(q, lo, n, dS.at[q], ddev)

    def y_q(q):
        lo = base(c, 1 - j, z) + NP
        arrived(q, lo, NQ, yQ.at[q], ydev)
        fwd(q, lo, NQ, dS.at[q], ddev)

    def y_p(q, d, back):
        lo = base(c, 1 - j, origin(d, back) if back else z)
        for at, m, u in ((lo, 4, 7), (lo + 4, NP - 4, 8)) if back == 4 else ((lo, NP, 2 * back - 1 + d if back else 0),):
            arrived(q, at, m, yP.at[q, u], ydev)
            fwd(q, at, m, dS.at[q], ddev)

    def m_at(zz, n=4):
        return M.at[pl.ds(zz * 4, n)]

    at = pl.ds(z * 4 + c * 2 + j, 1)
    send(M.at[at], M.at[at], mS, mY, ydev)
    start_y(0)
    start_z(0)
    got(M.at[pl.ds(z * 4 + c * 2 + (1 - j), 1)], mS, mY, ydev)
    both = M.at[pl.ds(z * 4 + c * 2, 2)]
    send(both, both, mS, mD, ddev)
    got(M.at[pl.ds(z * 4 + (1 - c) * 2, 2)], mS, mD, ddev)
    for d in (0, 1):
        send(m_at(z), m_at(z), mS, mZ.at[d, 0], zdev[d])

    def meta_relay(s):
        for d in (0, 1):
            if d == 1 and s == 4:
                continue
            at = m_at(origin(d, s))
            got(at, mS, mZ.at[d, s - 1], zdev[1 - d])
            if s + d < 4:
                send(at, at, mS, mZ.at[d, s], zdev[d])

    tok_cp.wait()

    def norm_rows(i, carry):
        rows = pl.ds(pl.multiple_of(i * 16, 16), 16)
        t = tok[rows, :].astype(F32)
        t = t - jnp.mean(t, axis=1, keepdims=True)
        var = jnp.mean(t * t, axis=1, keepdims=True)
        t = t * (1.0 / jnp.sqrt(var + 1e-05))
        normed[rows, :] = (t * gain[...][None] + beta[...][None]).astype(BF16)
        return carry

    lax.fori_loop(0, ROWS // 16, norm_rows, 0)
    zero_tile = jnp.zeros((TB, TB), BF16)
    G1[TOT] = zero_tile
    G2[TOT] = zero_tile

    y_q(0)
    a_step(0, 1)
    q_own(0)
    meta_relay(1)
    y_p(0, 0, 0)
    a_step(0, 2)
    meta_relay(2)
    q_step(0, 1)
    y_p(0, 0, 1)
    y_p(0, 1, 1)
    a_step(0, 3)
    start_y(1)
    meta_relay(3)
    q_step(0, 2)
    y_p(0, 0, 2)
    y_p(0, 1, 2)
    a_step(0, 4)
    start_z(1)
    meta_relay(4)

    m_id = lax.broadcasted_iota(jnp.int32, (32, TB), 0)
    first = ((m_id // 2 % 2) * 16 + (m_id % 2) * 8 + m_id // 4) * SLOTS
    lane = lax.broadcasted_iota(jnp.int32, (32, TB), 1)
    for q, (nr, nc) in enumerate(((RB, CB), (CB, RB))):
        listed = M[:, q, :]
        for s in range(SLOTS):
            W[s] = jnp.broadcast_to(listed[:, s : s + 1], (32, TB))

        def row(r, carry):
            want = jnp.where(lane < nc, r * nc + lane, -2)
            best = jnp.full((32, TB), -1, jnp.int32)
            for s in range(SLOTS):
                best = jnp.where(W[s] == want, first + s, best)
            best = jnp.max(best, axis=0, keepdims=True)
            Tv[q, pl.ds(r, 1), :] = jnp.where(best < 0, TOT, best)
            return carry

        lax.fori_loop(0, nr, row, 0)
    tab_cp = pltpu.make_async_copy(Tv, Ts, ls.at[4])
    tab_cp.start()
    q_step(0, 3)
    y_p(0, 0, 3)
    y_p(0, 1, 3)
    q_step(0, 4)
    y_p(0, 0, 4)
    y_q(1)
    pltpu.make_async_copy(t1, G1.at[pl.ds(own, SLOTS)], ls.at[0]).wait()
    arrived(0, base(1 - c, 0, 0), TOT // 2, dS.at[0], ddev)
    tab_cp.wait()

    def block(g, q, r, col, wide):
        cols = []
        for w in range(wide):
            cols.append(jnp.concatenate([g[Ts[q, r, col + w]], g[Ts[q, r + 1, col + w]]], axis=0))
        return cols[0] if wide == 1 else jnp.concatenate(cols, axis=1)

    def product(src, g, q, chunks, col, wide):
        acc = None
        for k in range(chunks):
            part = jnp.dot(
                src[:, k * 256 : (k + 1) * 256], block(g, q, 2 * k, col, wide),
                preferred_element_type=F32,
            )
            acc = part if acc is None else acc + part
        return acc

    def fc1(p, carry):
        acc = product(normed, G1, 0, RB // 2, 2 * p, 2)
        cols = pl.ds(pl.multiple_of(p * 256, 256), 256)
        hidden[:, cols] = jnp.maximum(acc + b1[cols][None], 0.0).astype(BF16)
        return carry

    a_step(1, 1)
    q_own(1)
    y_p(1, 0, 0)
    lax.fori_loop(0, 3, fc1, 0)
    a_step(1, 2)
    lax.fori_loop(3, 5, fc1, 0)
    q_step(1, 1)
    y_p(1, 0, 1)
    y_p(1, 1, 1)
    lax.fori_loop(5, 7, fc1, 0)
    a_step(1, 3)
    lax.fori_loop(7, 9, fc1, 0)
    q_step(1, 2)
    y_p(1, 0, 2)
    y_p(1, 1, 2)
    a_step(1, 4)
    q_step(1, 3)
    y_p(1, 0, 3)
    y_p(1, 1, 3)
    q_step(1, 4)
    y_p(1, 0, 4)
    pltpu.make_async_copy(t2, G2.at[pl.ds(own, SLOTS)], ls.at[1]).wait()
    arrived(1, base(1 - c, 0, 0), TOT // 2, dS.at[1], ddev)

    def fc2(early, i, carry):
        order = ((3, 0), (1, 1), (1, 0), (3, 1), (2, 0), (2, 1), (0, 0), (0, 1))
        off, d = jnp.int32(0), i % 2
        for at, (o, k) in enumerate(order):
            off = jnp.where(i == at, o, off)
            d = jnp.where(i == at, k, d)
        i = 2 * off + d
        share = d * 4 + (x + off) % 4
        pair, odd = share // 2 * 9, share % 2
        w = 0 if early else 2
        acc = product(hidden, G2, 1, CB // 2, pair + odd * 5 + w, 2).astype(BF16)
        S[i, w * ROWS : (w + 1) * ROWS] = acc[:, :TB]
        S[i, (w + 1) * ROWS : (w + 2) * ROWS] = acc[:, TB:]
        if early:
            return carry
        acc = product(hidden, G2, 1, CB // 2, pair + 4, 1)
        top, low = acc[: ROWS // 2], acc[ROWS // 2 :]
        left = lax.broadcasted_iota(jnp.int32, (ROWS // 2, TB), 1) < TB // 2
        turned = pltpu.roll(jnp.where(odd == 1, top, low), TB // 2, 1)
        half = jnp.where(left == (odd == 1), turned, jnp.where(odd == 1, low, top))
        S[i, 4 * ROWS :] = half.astype(BF16)
        return carry

    H = (SR - SB) // 2
    B = SB // 2

    def off_at(d, step):
        return (3 - step) if d == 0 else (1 + step) % 4

    def late_rows(h):
        return pl.ds(SB + h * H, H), pl.ds(h * H, H)

    def ring(step, h):
        for d in (0, 1):
            rows, slot = late_rows(h)
            at = S.at[2 * off_at(d, step) + d, rows]
            if step:
                old = R.at[d, step - 1, slot]
                got(old, rS, rX.at[d, step - 1, h], xdev[1 - d])
                at[...] = (at[...].astype(F32) + old[...].astype(F32)).astype(BF16)
            send(at, R.at[d, step, slot], rS, rX.at[d, step, h], xdev[d])

    def give(off):
        send(S.at[2 * off + 1 - yh, pl.ds(0, SB)], YB.at[off], rS, rB.at[off], hdev)

    def taken(off):
        got(YB.at[off], rS, rB.at[off], hdev)

    def ring_b(step, d):
        off, rows = jnp.where(d == 0, 3 - step, 1 + step), pl.ds(pl.multiple_of(d * B, B), B)
        at = S.at[2 * off + yh, rows]
        new = at[...].astype(F32) + YB[off, rows].astype(F32)
        if step:
            got(Q.at[d, step - 1], rS, rQ.at[d, step - 1], xdev[0])
            new = new + Q[d, step - 1].astype(F32)
        at[...] = new.astype(BF16)
        send(at, Q.at[d, step], rS, rQ.at[d, step], {"ffn": yh * 4 + (x + 1 + 2 * d) % 4})

    def late(first):
        lax.fori_loop(first, first + 2, functools.partial(fc2, False), 0)

    def early(first):
        lax.fori_loop(first, first + 2, functools.partial(fc2, True), 0)

    o = 1 - yh
    late(0)
    ring(0, 0)
    ring(0, 1)
    early(0)
    give(1 + 2 * yh)
    early(2)
    give(3 - 2 * yh)
    late(4)
    ring(1, 0)
    ring(1, 1)
    early(4)
    give(2)
    taken(3 - 2 * yh)
    ring_b(0, yh)
    late(2)
    ring(2, 0)
    early(6)
    give(0)
    taken(1 + 2 * yh)
    ring_b(0, o)
    ring(2, 1)
    late(6)
    taken(2)
    ring_b(1, yh)
    ring_b(1, o)
    for h in (0, 1):
        rows, slot = late_rows(h)
        at, old = S.at[o, rows], R.at[o, 2, slot]
        got(old, rS, rX.at[o, 2, h], xdev[0])
        at[...] = (at[...].astype(F32) + old[...].astype(F32)).astype(BF16)
        send(at, RY.at[slot], rS, rY.at[h], hdev)
    ring_b(2, yh)
    ring_b(2, o)
    taken(0)
    lo = pl.multiple_of((f // 2 * 9 + f % 2 * 4) * TB, TB)
    for h in (0, 1):
        rows, slot = late_rows(h)
        got(R.at[yh, 2, slot], rS, rX.at[yh, 2, h], xdev[0])
    late = S[yh, SB:].astype(F32) + R[yh, 2].astype(F32)
    early = S[yh, :SB].astype(F32) + YB[0].astype(F32)
    for d in (0, 1):
        got(Q.at[d, 2], rS, rQ.at[d, 2], xdev[1 - d])
    for h in (0, 1):
        rows, slot = late_rows(h)
        got(RY.at[slot], rS, rY.at[h], hdev)
    late = late + RY[...].astype(F32)
    main = [early[d * B : (d + 1) * B] + Q[d, 2].astype(F32) for d in (0, 1)]
    main += [late[w * ROWS : (w + 1) * ROWS] for w in (0, 1)]
    half = late[2 * ROWS :]
    turned = pltpu.roll(half, TB // 2, 1)

    @pl.when(f % 2 == 0)
    def _():
        full = jnp.concatenate(main + [jnp.concatenate([half, turned], axis=0)], axis=1)
        full = full + tok[:, pl.ds(lo, SW)].astype(F32)
        out[...] = (full[:, :576] + b2[...][None]).astype(BF16)

    @pl.when(f % 2 == 1)
    def _():
        full = jnp.concatenate([jnp.concatenate([turned, half], axis=0)] + main, axis=1)
        full = full + tok[:, pl.ds(lo, SW)].astype(F32)
        out[...] = (full[:, SW - 576 :] + b2[...][None]).astype(BF16)

    for q in (0, 1):
        all_sent = G[q].at[pl.ds(0, 372)]
        pltpu.make_async_remote_copy(
            src_ref=all_sent, dst_ref=all_sent, send_sem=ss.at[q], recv_sem=ss.at[q],
            device_id=ddev, device_id_type=MESH,
        ).wait_send()
    sent = S.at[pl.ds(0, 7)]
    pltpu.make_async_remote_copy(
        src_ref=sent, dst_ref=sent, send_sem=rS, recv_sem=rS, device_id=ddev, device_id_type=MESH,
    ).wait_send()
    ref = M.at[pl.ds(0, 31)]
    pltpu.make_async_remote_copy(
        src_ref=ref, dst_ref=ref, send_sem=mS, recv_sem=mS, device_id=ddev, device_id_type=MESH,
    ).wait_send()


def on_device(tokens, gain, beta, t1, i1, n1, b1, t2, i2, n2, b2):
    vm = pl.BlockSpec(memory_space=pltpu.VMEM)
    hb = pl.BlockSpec(memory_space=pl.ANY)
    sm = pl.BlockSpec(memory_space=pltpu.SMEM)
    dma, V = pltpu.SemaphoreType.DMA, pltpu.VMEM
    return pl.pallas_call(
        kernel,
        out_shape=jax.ShapeDtypeStruct((ROWS, 576), BF16),
        in_specs=[hb, vm, vm, vm, vm, hb, hb, sm, hb, sm, hb],
        out_specs=vm,
        scratch_shapes=[
            V((TOT + 1, TB, TB), BF16),
            V((TOT + 1, TB, TB), BF16),
            V((32, 8, TB), jnp.int32),
            V((2, 40, TB), jnp.int32),
            pltpu.SMEM((2, 40, TB), jnp.int32),
            V((ROWS, D), BF16),
            V((ROWS, D), BF16),
            V((ROWS, FFS), BF16),
            V((8, SR, TB), BF16),
            V((2, 3, SR - SB, TB), BF16),
            V((SR - SB, TB), BF16),
            V((4, SB, TB), BF16),
            V((2, 3, SB // 2, TB), BF16),
            V((SLOTS, 32, TB), jnp.int32),
            pltpu.SMEM((1, 1), jnp.int32),
            pltpu.SMEM((1, 1), jnp.int32),
            dma((7,)),
            dma((2,)),
            dma((2, 2, 4, 2)),
            dma((2, 2, 4, 2)),
            dma((2,)),
            dma((2, 9)),
            dma((2,)),
            dma,
            dma,
            dma,
            dma((2, 4)),
            dma,
            dma((2, 3, 2)),
            dma((2,)),
            dma((4,)),
            dma((2, 3)),
        ],
        compiler_params=pltpu.CompilerParams(
            collective_id=0, has_side_effects=True, vmem_limit_bytes=60 * 1024 * 1024
        ),
    )(
        tokens, gain, beta, b1, b2, t1.reshape(SLOTS, TB, TB), t2.reshape(SLOTS, TB, TB), i1, n1, i2, n2,
    )


def solution(mesh):
    tile, pair = P("blk", "ffn", None, None, None), P("blk", "ffn")
    placed = (
        P("blk", None), P(), P(), tile, P("blk", "ffn", None), pair, P("ffn"),
        tile, P("blk", "ffn", None), pair, P("ffn"),
    )
    return jax.shard_map(
        on_device, mesh=mesh, in_specs=placed, out_specs=P("blk", "ffn"), check_vma=False
    )
```

```python
import functools

import jax
import jax.numpy as jnp
from jax import lax
from jax.experimental import pallas as pl
from jax.experimental.pallas import tpu as pltpu
from jax.sharding import PartitionSpec as P

MESH = pl.DeviceIdType.MESH
TB = 128
SLOTS = 12
NP, NQ = 7, 5
FAR = (2, 3)
ROWS, D, FFS = 256, 4608, 2304
RB, CB = 36, 18
SR = 1152
SB = 512
TOT = 32 * SLOTS
F32, BF16 = jnp.float32, jnp.bfloat16


def kernel(
    tok_h, gain, beta, b1, b2, t1, t2, i1, c1, i2, c2, out,
    G1, G2, M, Tv, Ts, tok, normed, hidden, S, R, RY, YB, Q, W,
    ls, ss, zA, zQ, yQ, yP, dS, mS, mY, mD, mZ, rS, rX, rY, rB, rQ,
):
    b = lax.axis_index("blk")
    f = lax.axis_index("ffn")
    j, z, c = b // 16, (b // 2) % 8, b % 2
    yh, x = f // 4, f % 4
    tin, G = (t1, t2), (G1, G2)
    zdev = tuple({"blk": j * 16 + ((z + dz) % 8) * 2 + c} for dz in (1, 7))
    ydev = {"blk": (1 - j) * 16 + z * 2 + c}
    ddev = {"blk": j * 16 + z * 2 + (1 - c)}
    xdev = tuple({"ffn": yh * 4 + (x + dx) % 4} for dx in (1, 3))
    hdev = {"ffn": (1 - yh) * 4 + x}

    bar = pltpu.get_barrier_semaphore()
    for dev in (hdev, *xdev, *zdev, ydev, ddev):
        pl.semaphore_signal(bar, inc=1, device_id=dev, device_id_type=MESH)
    tok_cp = pltpu.make_async_copy(tok_h, tok, ls.at[2])
    tok_cp.start()
    sub = lax.broadcasted_iota(jnp.int32, (8, TB), 0)
    lane8 = lax.broadcasted_iota(jnp.int32, (8, TB), 1)
    seen = jnp.full((8, TB), -1, jnp.int32)
    for q, (idx, num) in enumerate(((i1, c1), (i2, c2))):
        live = lane8 < jnp.broadcast_to(num[...], (8, TB))
        for s in range(SLOTS):
            here = (sub == q) & (lane8 == s) & live
            seen = jnp.where(here, idx[0, 0, s], seen)
    M[z * 4 + c * 2 + j] = seen
    pl.semaphore_wait(bar, 7)

    def send(src, dst, s_sem, r_sem, dev):
        pltpu.make_async_remote_copy(
            src_ref=src, dst_ref=dst, send_sem=s_sem, recv_sem=r_sem,
            device_id=dev, device_id_type=MESH,
        ).start()

    def got(ref, s_sem, r_sem, dev):
        pltpu.make_async_remote_copy(
            src_ref=ref, dst_ref=ref, send_sem=s_sem, recv_sem=r_sem,
            device_id=dev, device_id_type=MESH,
        ).wait_recv()

    def base(cc, jj, zz):
        return (cc * 16 + jj * 8 + zz) * SLOTS

    own = base(c, j, z)

    def start_y(q):
        g, t = G[q], tin[q]
        send(t.at[pl.ds(NP, NQ)], g.at[pl.ds(own + NP, NQ)], ss.at[q], yQ.at[q], ydev)
        send(t.at[pl.ds(0, NP)], g.at[pl.ds(own, NP)], ss.at[q], yP.at[q, 0], ydev)

    def start_z(q):
        g, t = G[q], tin[q]
        for k, (lo, n) in enumerate(((0, NP), (NP, NQ))):
            for d in (0, 1):
                send(t.at[pl.ds(lo, n)], g.at[pl.ds(own + lo, n)], ss.at[q], zA.at[q, d, 0, k], zdev[d])
        send(t, g.at[pl.ds(own, SLOTS)], ss.at[q], dS.at[q], ddev)
        pltpu.make_async_copy(t, g.at[pl.ds(own, SLOTS)], ls.at[q]).start()

    def origin(d, s):
        return (z + (8 - s if d == 0 else s)) % 8

    def fwd(q, lo, n, r_sem, dev):
        ref = G[q].at[pl.ds(lo, n)]
        send(ref, ref, ss.at[q], r_sem, dev)

    def arrived(q, lo, n, r_sem, dev):
        got(G[q].at[pl.ds(lo, n)], ss.at[q], r_sem, dev)

    def a_part(q, d, s, k):
        lo, n = base(c, j, origin(d, s)) + (NP if k else 0), (NQ if k else NP)
        far = ((lo, 4, 0), (lo + 4, n - 4, 1)) if d == k == 0 else ((lo, n, k),)
        if s == 4:
            for at, m, u in far:
                arrived(q, at, m, zA.at[q, d, 3, u], zdev[1 - d])
                if not k:
                    fwd(q, at, m, yP.at[q, 7 + u], ydev)
                fwd(q, at, m, dS.at[q], ddev)
            return
        arrived(q, lo, n, zA.at[q, d, s - 1, k], zdev[1 - d])
        if s < 3:
            fwd(q, lo, n, zA.at[q, d, s, k], zdev[d])
        elif d == k:
            for at, m, u in far:
                fwd(q, at, m, zA.at[q, d, 3, u], zdev[d])
        if not k:
            fwd(q, lo, n, yP.at[q, 2 * s - 1 + d], ydev)
        fwd(q, lo, n, dS.at[q], ddev)

    def a_step(q, s):
        for k in (0, 1):
            for d in (0, 1):
                if s < 4 or d == k:
                    a_part(q, d, s, k)

    def q_at(d, s, half):
        lo = base(c, 1 - j, origin(d, s)) + NP
        if half is None:
            return lo, NQ
        return (lo, FAR[0]) if d != half else (lo + FAR[0], FAR[1])

    def q_own(q):
        lo = base(c, 1 - j, z) + NP
        for d in (0, 1):
            fwd(q, lo, NQ, zQ.at[q, d, 0, 0], zdev[d])

    def q_step(q, s):
        for half in (1, 0) if s == 3 else (1,) if s == 4 else (None,):
            for d in (0, 1):
                lo, n = q_at(d, s, half)
                arrived(q, lo, n, zQ.at[q, d, s - 1, 1 if half == 0 else 0], zdev[1 - d])
                if s == 1:
                    fwd(q, lo, n, zQ.at[q, d, 1, 0], zdev[d])
                if s == 2:
                    for h in (1, 0):
                        lo2, n2 = q_at(d, s, h)
                        fwd(q, lo2, n2, zQ.at[q, d, 2, 1 - h], zdev[d])
                if s == 3 and half == 1:
                    fwd(q, lo, n, zQ.at[q, d, 3, 0], zdev[d])
                fwd(q, lo, n, dS.at[q], ddev)

    def y_q(q):
        lo = base(c, 1 - j, z) + NP
        arrived(q, lo, NQ, yQ.at[q], ydev)
        fwd(q, lo, NQ, dS.at[q], ddev)

    def y_p(q, d, back):
        lo = base(c, 1 - j, origin(d, back) if back else z)
        for at, m, u in ((lo, 4, 7), (lo + 4, NP - 4, 8)) if back == 4 else ((lo, NP, 2 * back - 1 + d if back else 0),):
            arrived(q, at, m, yP.at[q, u], ydev)
            fwd(q, at, m, dS.at[q], ddev)

    def m_at(zz, n=4):
        return M.at[pl.ds(zz * 4, n)]

    at = pl.ds(z * 4 + c * 2 + j, 1)
    send(M.at[at], M.at[at], mS, mY, ydev)
    start_y(0)
    start_z(0)
    got(M.at[pl.ds(z * 4 + c * 2 + (1 - j), 1)], mS, mY, ydev)
    both = M.at[pl.ds(z * 4 + c * 2, 2)]
    send(both, both, mS, mD, ddev)
    got(M.at[pl.ds(z * 4 + (1 - c) * 2, 2)], mS, mD, ddev)
    for d in (0, 1):
        send(m_at(z), m_at(z), mS, mZ.at[d, 0], zdev[d])

    def meta_relay(s):
        for d in (0, 1):
            if d == 1 and s == 4:
                continue
            at = m_at(origin(d, s))
            got(at, mS, mZ.at[d, s - 1], zdev[1 - d])
            if s + d < 4:
                send(at, at, mS, mZ.at[d, s], zdev[d])

    tok_cp.wait()

    def norm_rows(i, carry):
        rows = pl.ds(pl.multiple_of(i * 16, 16), 16)
        t = tok[rows, :].astype(F32)
        t = t - jnp.mean(t, axis=1, keepdims=True)
        var = jnp.mean(t * t, axis=1, keepdims=True)
        t = t * (1.0 / jnp.sqrt(var + 1e-05))
        normed[rows, :] = (t * gain[...][None] + beta[...][None]).astype(BF16)
        return carry

    def norm_quarter(k):
        lax.fori_loop(4 * k, 4 * k + 4, norm_rows, 0)

    zero_tile = jnp.zeros((TB, TB), BF16)
    G1[TOT] = zero_tile
    G2[TOT] = zero_tile

    norm_quarter(0)
    y_q(0)
    a_step(0, 1)
    q_own(0)
    meta_relay(1)
    norm_quarter(1)
    y_p(0, 0, 0)
    a_step(0, 2)
    meta_relay(2)
    norm_quarter(2)
    q_step(0, 1)
    y_p(0, 0, 1)
    y_p(0, 1, 1)
    a_step(0, 3)
    start_y(1)
    meta_relay(3)
    norm_quarter(3)
    q_step(0, 2)
    y_p(0, 0, 2)
    y_p(0, 1, 2)
    a_step(0, 4)
    start_z(1)
    meta_relay(4)

    m_id = lax.broadcasted_iota(jnp.int32, (32, TB), 0)
    first = ((m_id // 2 % 2) * 16 + (m_id % 2) * 8 + m_id // 4) * SLOTS
    lane = lax.broadcasted_iota(jnp.int32, (32, TB), 1)
    for q, (nr, nc) in enumerate(((RB, CB), (CB, RB))):
        listed = M[:, q, :]
        for s in range(SLOTS):
            W[s] = jnp.broadcast_to(listed[:, s : s + 1], (32, TB))

        def row(r, carry):
            want = jnp.where(lane < nc, r * nc + lane, -2)
            best = jnp.full((32, TB), -1, jnp.int32)
            for s in range(SLOTS):
                best = jnp.where(W[s] == want, first + s, best)
            best = jnp.max(best, axis=0, keepdims=True)
            Tv[q, pl.ds(r, 1), :] = jnp.where(best < 0, TOT, best)
            return carry

        lax.fori_loop(0, nr, row, 0)
    tab_cp = pltpu.make_async_copy(Tv, Ts, ls.at[4])
    tab_cp.start()
    q_step(0, 3)
    y_p(0, 0, 3)
    y_p(0, 1, 3)
    q_step(0, 4)
    y_p(0, 0, 4)
    y_q(1)
    pltpu.make_async_copy(t1, G1.at[pl.ds(own, SLOTS)], ls.at[0]).wait()
    arrived(0, base(1 - c, 0, 0), TOT // 2, dS.at[0], ddev)
    tab_cp.wait()

    def block(g, q, r, col, wide):
        cols = []
        for w in range(wide):
            cols.append(jnp.concatenate([g[Ts[q, r, col + w]], g[Ts[q, r + 1, col + w]]], axis=0))
        return cols[0] if wide == 1 else jnp.concatenate(cols, axis=1)

    def product(src, g, q, chunks, col, wide):
        acc = None
        for k in range(chunks):
            part = jnp.dot(
                src[:, k * 256 : (k + 1) * 256], block(g, q, 2 * k, col, wide),
                preferred_element_type=F32,
            )
            acc = part if acc is None else acc + part
        return acc

    def fc1(p, carry):
        acc = product(normed, G1, 0, RB // 2, 2 * p, 2)
        cols = pl.ds(pl.multiple_of(p * 256, 256), 256)
        hidden[:, cols] = jnp.maximum(acc + b1[cols][None], 0.0).astype(BF16)
        return carry

    a_step(1, 1)
    q_own(1)
    y_p(1, 0, 0)
    lax.fori_loop(0, 3, fc1, 0)
    a_step(1, 2)
    lax.fori_loop(3, 5, fc1, 0)
    q_step(1, 1)
    y_p(1, 0, 1)
    y_p(1, 1, 1)
    lax.fori_loop(5, 7, fc1, 0)
    a_step(1, 3)
    lax.fori_loop(7, 9, fc1, 0)
    q_step(1, 2)
    y_p(1, 0, 2)
    y_p(1, 1, 2)
    a_step(1, 4)
    q_step(1, 3)
    y_p(1, 0, 3)
    y_p(1, 1, 3)
    q_step(1, 4)
    y_p(1, 0, 4)
    pltpu.make_async_copy(t2, G2.at[pl.ds(own, SLOTS)], ls.at[1]).wait()
    arrived(1, base(1 - c, 0, 0), TOT // 2, dS.at[1], ddev)

    def half_block(v, odd):
        top, low = v[: ROWS // 2], v[ROWS // 2 :]
        left = lax.broadcasted_iota(jnp.int32, (ROWS // 2, TB), 1) < TB // 2
        turned = pltpu.roll(jnp.where(odd == 1, top, low), TB // 2, 1)
        return jnp.where(left == (odd == 1), turned, jnp.where(odd == 1, low, top))

    def fc2(early, i, carry):
        order = ((3, 0), (1, 1), (1, 0), (3, 1), (2, 0), (2, 1), (0, 0), (0, 1))
        off, d = jnp.int32(0), i % 2
        for at, (o, k) in enumerate(order):
            off = jnp.where(i == at, o, off)
            d = jnp.where(i == at, k, d)
        i = 2 * off + d
        share = d * 4 + (x + off) % 4
        pair, odd = share // 2 * 9, share % 2
        w = 0 if early else 2
        acc = product(hidden, G2, 1, CB // 2, pair + odd * 5 + w, 2).astype(BF16)
        S[i, w * ROWS : (w + 1) * ROWS] = acc[:, :TB]
        S[i, (w + 1) * ROWS : (w + 2) * ROWS] = acc[:, TB:]
        if early:
            return carry
        acc = product(hidden, G2, 1, CB // 2, pair + 4, 1)
        S[i, 4 * ROWS :] = half_block(acc, odd).astype(BF16)
        return carry

    H = (SR - SB) // 2
    B = SB // 2

    def off_at(d, step):
        return (3 - step) if d == 0 else (1 + step) % 4

    def late_rows(h):
        return pl.ds(SB + h * H, H), pl.ds(h * H, H)

    def ring(step, h):
        for d in (0, 1):
            rows, slot = late_rows(h)
            at = S.at[2 * off_at(d, step) + d, rows]
            if step:
                old = R.at[d, step - 1, slot]
                got(old, rS, rX.at[d, step - 1, h], xdev[1 - d])
                at[...] = (at[...].astype(F32) + old[...].astype(F32)).astype(BF16)
            send(at, R.at[d, step, slot], rS, rX.at[d, step, h], xdev[d])

    def give(off):
        send(S.at[2 * off + 1 - yh, pl.ds(0, SB)], YB.at[off], rS, rB.at[off], hdev)

    def taken(off):
        got(YB.at[off], rS, rB.at[off], hdev)

    def ring_b(step, d):
        off, rows = jnp.where(d == 0, 3 - step, 1 + step), pl.ds(pl.multiple_of(d * B, B), B)
        at = S.at[2 * off + yh, rows]
        new = at[...].astype(F32) + YB[off, rows].astype(F32)
        if step:
            got(Q.at[d, step - 1], rS, rQ.at[d, step - 1], xdev[0])
            new = new + Q[d, step - 1].astype(F32)
        at[...] = new.astype(BF16)
        send(at, Q.at[d, step], rS, rQ.at[d, step], {"ffn": yh * 4 + (x + 1 + 2 * d) % 4})

    def late(first):
        lax.fori_loop(first, first + 2, functools.partial(fc2, False), 0)

    def early(first):
        lax.fori_loop(first, first + 2, functools.partial(fc2, True), 0)

    o = 1 - yh
    late(0)
    ring(0, 0)
    ring(0, 1)
    early(0)
    give(1 + 2 * yh)
    early(2)
    give(3 - 2 * yh)
    late(4)
    ring(1, 0)
    ring(1, 1)
    early(4)
    give(2)
    taken(3 - 2 * yh)
    ring_b(0, yh)
    late(2)
    ring(2, 0)
    early(6)
    give(0)
    taken(1 + 2 * yh)
    ring_b(0, o)
    ring(2, 1)
    late(6)
    taken(2)
    ring_b(1, yh)
    ring_b(1, o)
    for h in (0, 1):
        rows, slot = late_rows(h)
        at, old = S.at[o, rows], R.at[o, 2, slot]
        got(old, rS, rX.at[o, 2, h], xdev[0])
        at[...] = (at[...].astype(F32) + old[...].astype(F32)).astype(BF16)
        send(at, RY.at[slot], rS, rY.at[h], hdev)
    ring_b(2, yh)
    ring_b(2, o)
    taken(0)
    first = f // 2 * 9

    def residual(w):
        if w < 4:
            return tok[:, pl.ds(pl.multiple_of((first + f % 2 * 5 + w) * TB, TB), TB)].astype(F32)
        return half_block(tok[:, pl.ds(pl.multiple_of((first + 4) * TB, TB), TB)].astype(F32), f % 2)

    def finish(sums, at, shared):
        e = b2[...][None]
        for w, v in sums.items():
            if w < 4:
                out[at + w * TB : at + (w + 1) * TB, :] = (v + e[:, at + w * TB : at + (w + 1) * TB]).astype(BF16).T
            else:
                twice = jnp.concatenate([e[:, shared : shared + TB // 2]] * 2, axis=1)
                v = (v + twice).astype(BF16).T
                out[shared : shared + TB // 2, : ROWS // 2] = v[: TB // 2]
                out[shared : shared + TB // 2, ROWS // 2 :] = v[TB // 2 :]

    def finish_either(sums):
        pl.when(f % 2 == 0)(lambda: finish(sums, 0, 4 * TB))
        pl.when(f % 2 == 1)(lambda: finish(sums, TB // 2, 0))

    for h in (0, 1):
        rows, slot = late_rows(h)
        got(R.at[yh, 2, slot], rS, rX.at[yh, 2, h], xdev[0])
        got(RY.at[slot], rS, rY.at[h], hdev)
    sums = {}
    for w in (2, 3, 4):
        n = ROWS if w < 4 else ROWS // 2
        rows, slot = pl.ds(w * ROWS, n), pl.ds(w * ROWS - SB, n)
        sums[w] = S[yh, rows].astype(F32) + R[yh, 2, slot].astype(F32) + RY[slot].astype(F32) + residual(w)
    finish_either(sums)
    for d in (0, 1):
        got(Q.at[d, 2], rS, rQ.at[d, 2], xdev[1 - d])
    sums = {}
    for w in (0, 1):
        rows = pl.ds(w * ROWS, ROWS)
        sums[w] = S[yh, rows].astype(F32) + YB[0, rows].astype(F32) + Q[w, 2].astype(F32) + residual(w)
    finish_either(sums)

    for q in (0, 1):
        all_sent = G[q].at[pl.ds(0, 372)]
        pltpu.make_async_remote_copy(
            src_ref=all_sent, dst_ref=all_sent, send_sem=ss.at[q], recv_sem=ss.at[q],
            device_id=ddev, device_id_type=MESH,
        ).wait_send()
    sent = S.at[pl.ds(0, 7)]
    pltpu.make_async_remote_copy(
        src_ref=sent, dst_ref=sent, send_sem=rS, recv_sem=rS, device_id=ddev, device_id_type=MESH,
    ).wait_send()
    ref = M.at[pl.ds(0, 31)]
    pltpu.make_async_remote_copy(
        src_ref=ref, dst_ref=ref, send_sem=mS, recv_sem=mS, device_id=ddev, device_id_type=MESH,
    ).wait_send()


def on_device(tokens, gain, beta, t1, i1, n1, b1, t2, i2, n2, b2):
    vm = pl.BlockSpec(memory_space=pltpu.VMEM)
    hb = pl.BlockSpec(memory_space=pl.ANY)
    sm = pl.BlockSpec(memory_space=pltpu.SMEM)
    dma, V = pltpu.SemaphoreType.DMA, pltpu.VMEM
    return pl.pallas_call(
        kernel,
        out_shape=jax.ShapeDtypeStruct((576, ROWS), BF16),
        in_specs=[hb, vm, vm, vm, vm, hb, hb, sm, vm, sm, vm],
        out_specs=vm,
        scratch_shapes=[
            V((TOT + 1, TB, TB), BF16),
            V((TOT + 1, TB, TB), BF16),
            V((32, 8, TB), jnp.int32),
            V((2, 40, TB), jnp.int32),
            pltpu.SMEM((2, 40, TB), jnp.int32),
            V((ROWS, D), BF16),
            V((ROWS, D), BF16),
            V((ROWS, FFS), BF16),
            V((8, SR, TB), BF16),
            V((2, 3, SR - SB, TB), BF16),
            V((SR - SB, TB), BF16),
            V((4, SB, TB), BF16),
            V((2, 3, SB // 2, TB), BF16),
            V((SLOTS, 32, TB), jnp.int32),
            dma((5,)),
            dma((2,)),
            dma((2, 2, 4, 2)),
            dma((2, 2, 4, 2)),
            dma((2,)),
            dma((2, 9)),
            dma((2,)),
            dma,
            dma,
            dma,
            dma((2, 4)),
            dma,
            dma((2, 3, 2)),
            dma((2,)),
            dma((4,)),
            dma((2, 3)),
        ],
        compiler_params=pltpu.CompilerParams(
            collective_id=0, has_side_effects=True, vmem_limit_bytes=60 * 1024 * 1024
        ),
    )(
        tokens, gain, beta, b1, b2, t1.reshape(SLOTS, TB, TB), t2.reshape(SLOTS, TB, TB), i1, n1, i2, n2,
    ).T


def solution(mesh):
    tile, pair = P("blk", "ffn", None, None, None), P("blk", "ffn")
    placed = (
        P("blk", None), P(), P(), tile, P("blk", "ffn", None), pair, P("ffn"),
        tile, P("blk", "ffn", None), pair, P("ffn"),
    )
    return jax.shard_map(
        on_device, mesh=mesh, in_specs=placed, out_specs=P("blk", "ffn"), check_vma=False
    )
```
